32 devices in a mesh: dp: 8 (over y, x, core), hid: 4 (over z).
Axes of the slice: x: 2, y: 2, z: 4, core: 2. Of those that a mesh axis runs over, the one named last changes fastest.
Arguments:
- tokens: bfloat16 [4096, 8192], P('dp', 'hid'), may hold values from -6 to 6
- up_blocks: bfloat16 [7, 64, 128, 1024], P(None, 'hid', 'dp'), may hold values from -0.1875 to 0.1875
- up_left: bfloat16 [8192, 512], P('hid'), may hold values from -0.0625 to 0.0625
- up_right: bfloat16 [512, 65536], P(None, 'hid'), may hold values from -0.25 to 0.25
- down_blocks: bfloat16 [7, 64, 1024, 128], P(None, 'hid', 'dp'), may hold values from -0.0625 to 0.0625
- down_left: bfloat16 [65536, 512], P('hid'), may hold values from -0.0234375 to 0.0234375
- down_right: bfloat16 [512, 8192], P(None, 'hid'), may hold values from -0.25 to 0.25
Outputs:
- mixed: bfloat16 [4096, 8192], P('dp', 'hid')
The draws below stay inside these ranges and needn't reach their ends.
All inputs are finite; a program needn't handle non-finite values.
Results may differ from the reference program's by a relative error of at most 0.0059.
Values may be sent and summed in bfloat16 or wider, within the bound.
A program may use at most 384 MiB of HBM per device.

```python
import jax
import jax.numpy as jnp
from jax import lax

D = 8192
FFH = 65536
BLK = 128
R = 512
NT = 7
TOK_DEV = 512
TOKENS = 4096


def steps_of(rng, extent, shards, least, largest):
    level = 1.0
    for dim, shards_of in shards:
        steps = jax.random.uniform(jax.random.fold_in(jax.random.fold_in(rng, 6), dim), (shards_of,), jnp.float32, least / len(shards), largest / len(shards))
        level = level * jnp.repeat(jnp.exp(steps), extent[dim] // shards_of).reshape((-1,) + (1,) * (len(extent) - 1 - dim))
    return level


def normal_values(stream_key, dims, spread, limit, cuts=(), held_as=jnp.bfloat16):
    values = spread * jax.random.normal(stream_key, dims, jnp.float32)
    if cuts:
        values = values * steps_of(stream_key, dims, cuts, -0.22, 0.18)
    return jnp.clip(values, -limit, limit).astype(held_as)


def setup_inputs(seed: int = 0) -> dict:
    splits = jax.random.split(jax.random.key(seed), 8)
    tokens = normal_values(splits[0], (TOKENS, D), 1.0, 6.0, ((0, 8), (1, 4)))
    up_blocks = normal_values(splits[1], (NT, D // BLK, BLK, FFH // D * BLK), (NT * BLK) ** -0.5, 0.1875, ((1, 4), (2, 8)))
    up_left = normal_values(splits[2], (D, R), D ** -0.5, 0.0625, ((0, 4),))
    up_right = normal_values(splits[3], (R, FFH), R ** -0.5, 0.25, ((1, 4),))
    down_blocks = normal_values(splits[4], (NT, D // BLK, FFH // D * BLK, BLK), (NT * (FFH // D) * BLK) ** -0.5, 0.0625, ((1, 4), (2, 8)))
    down_left = normal_values(splits[5], (FFH, R), FFH ** -0.5, 0.0234375, ((0, 4),))
    down_right = normal_values(splits[6], (R, D), R ** -0.5, 0.25, ((1, 4),))
    return {"tokens": tokens, "up_blocks": up_blocks, "up_left": up_left, "up_right": up_right, "down_blocks": down_blocks, "down_left": down_left, "down_right": down_right}


def term_offset(step_index):
    return 0 if step_index == 0 else 2 ** (step_index - 1)


def reference(tokens, up_blocks, up_left, up_right, down_blocks, down_left, down_right):
    block_count = D // BLK
    group_width = FFH // D * BLK

    def token_block(token_rows):
        row_count = token_rows.shape[0]
        pieces = token_rows.reshape(row_count, block_count, BLK).astype(jnp.float32)
        block_order = jnp.arange(block_count, dtype=jnp.int32)
        hidden_sum = jnp.zeros((row_count, block_count, group_width), jnp.float32)
        for step_index in range(NT):
            source = pieces[:, jnp.bitwise_xor(block_order, term_offset(step_index)), :]
            hidden_sum = hidden_sum + jnp.einsum("abk,bkn->abn", source, up_blocks[step_index].astype(jnp.float32))
        rank_up = jnp.dot(token_rows, up_left, preferred_element_type=jnp.float32).astype(jnp.bfloat16)
        pre_activation = hidden_sum.reshape(row_count, FFH) + jnp.dot(rank_up, up_right, preferred_element_type=jnp.float32)
        active = jax.nn.gelu(pre_activation, approximate=False).astype(jnp.bfloat16)
        grouped = active.reshape(row_count, block_count, group_width).astype(jnp.float32)
        out_sum = jnp.zeros((row_count, block_count, BLK), jnp.float32)
        for step_index in range(NT):
            contribution = jnp.einsum("abn,bnk->abk", grouped, down_blocks[step_index].astype(jnp.float32))
            out_sum = out_sum + contribution[:, jnp.bitwise_xor(block_order, term_offset(step_index)), :]
        rank_down = jnp.dot(active, down_left, preferred_element_type=jnp.float32).astype(jnp.bfloat16)
        result = out_sum.reshape(row_count, D) + jnp.dot(rank_down, down_right, preferred_element_type=jnp.float32)
        return result.astype(jnp.bfloat16)

    blocked = tokens.reshape(TOKENS // TOK_DEV, TOK_DEV, D)
    return lax.map(token_block, blocked).reshape(TOKENS, D)
```

```python
import functools

import jax
import jax.numpy as jnp
from jax import lax
from jax.experimental import pallas as pl
from jax.experimental.pallas import tpu as pltpu
from jax.sharding import PartitionSpec as P


def from_partner(block, axis, stride):
    count = lax.axis_size(axis)
    route = []
    for low in range(count):
        high = low | 1 << stride
        if high != low and high < count:
            route += [(low, high), (high, low)]
    return lax.ppermute(block, axis, route)


def swap_blocks(values, block_span, along_axis):
    full_shape = values.shape
    extent = full_shape[along_axis]
    split_shape = (
        full_shape[:along_axis]
        + (extent // (2 * block_span), 2, block_span)
        + full_shape[along_axis + 1 :]
    )
    return jnp.flip(values.reshape(split_shape), along_axis + 1).reshape(full_shape)


def shards_plain(tokens, up_blocks, up_left, up_right, down_blocks, down_left, down_right):
    token_rows = tokens.shape[0]
    local_blocks = up_blocks.shape[1]
    block_size = down_blocks.shape[3]
    term_count = up_blocks.shape[0]
    pieces = tokens.reshape(token_rows, local_blocks, block_size)
    sources = []
    for step_index in range(term_count):
        block_span = 0 if step_index == 0 else 2 ** (step_index - 1)
        if block_span == 0:
            sources.append(pieces)
        elif block_span < local_blocks:
            sources.append(swap_blocks(pieces, block_span, 1))
        else:
            swap_bit = (block_span // local_blocks).bit_length() - 1
            partner_rows = from_partner(tokens, "hid", swap_bit)
            sources.append(partner_rows.reshape(token_rows, local_blocks, block_size))
    stacked = jnp.stack(sources)
    up_full = lax.all_gather(up_blocks, "dp", axis=2, tiled=True)
    hidden_sum = jnp.einsum("tabk,tbkn->abn", stacked, up_full, preferred_element_type=jnp.float32)
    down_full = lax.all_gather(down_blocks, "dp", axis=2, tiled=True)
    rank_up = lax.psum(jnp.dot(tokens, up_left, preferred_element_type=jnp.float32), "hid").astype(
        jnp.bfloat16
    )
    pre_activation = hidden_sum.reshape(
        token_rows, hidden_sum.shape[1] * hidden_sum.shape[2]
    ) + jnp.dot(rank_up, up_right, preferred_element_type=jnp.float32)
    active = jax.nn.gelu(pre_activation, approximate=False).astype(jnp.bfloat16)
    grouped = active.reshape(token_rows, local_blocks, hidden_sum.shape[2])
    contributions = jnp.einsum(
        "abn,tbnk->tabk", grouped, down_full, preferred_element_type=jnp.float32
    )
    out_sum = jnp.zeros((token_rows, local_blocks, block_size), jnp.float32)
    for step_index in range(term_count):
        block_span = 0 if step_index == 0 else 2 ** (step_index - 1)
        if block_span == 0:
            out_sum = contributions[0]
        elif block_span < local_blocks:
            out_sum = out_sum + swap_blocks(contributions[step_index], block_span, 1)
        else:
            swap_bit = (block_span // local_blocks).bit_length() - 1
            out_sum = out_sum + from_partner(contributions[step_index], "hid", swap_bit)
    rank_down = lax.psum(
        jnp.dot(active, down_left, preferred_element_type=jnp.float32), "hid"
    ).astype(jnp.bfloat16)
    result = out_sum.reshape(token_rows, local_blocks * block_size) + jnp.dot(
        rank_down, down_right, preferred_element_type=jnp.float32
    )
    return result.astype(jnp.bfloat16)


GROUPS = 2
AHEAD = 4
MESH = pl.DeviceIdType.MESH


def flip(index, bit):
    return index + bit - 2 * bit * ((index // bit) % 2)


def fused(
    tokens, up_blocks, up_left, up_right, down_blocks, down_left, down_right,
    out, up_all, down_all,
    tok, swapped, left, right, rank, rank_part, rank_in, active, acc, give, take,
    w_up, w_right, w_down, w_left,
    sent, got, tok_sent, tok_got, give_sent, give_got,
    rs_sent, rs_got, ag_sent, ag_got, own_sem, load_sem, pre_sem,
):
    rows = tokens.shape[0]
    terms, blocks = up_blocks.shape[0], up_blocks.shape[1]
    size = down_blocks.shape[3]
    width = up_blocks.shape[3]
    depth = terms * size
    units = blocks // GROUPS
    me, here = lax.axis_index("dp"), lax.axis_index("hid")
    slabs = lax.axis_size("hid")
    bits = slabs.bit_length() - 1
    locals_ = terms - bits
    share = rows // slabs
    sibling, across, beside = flip(me, 1), flip(me, 2), flip(me, 4)
    chunk = GROUPS * size

    barrier = pltpu.get_barrier_semaphore()
    for near in (sibling, across, beside):
        pl.semaphore_signal(barrier, inc=1, device_id=(near, here), device_id_type=MESH)
    for k in range(1, slabs):
        pl.semaphore_signal(
            barrier, inc=1, device_id=(me, (here + k) % slabs), device_id_type=MESH
        )
    pl.semaphore_wait(barrier, 3 + slabs - 1)

    stages = ((up_blocks, up_all), (down_blocks, down_all))

    def remote(source, target, send, recv, device):
        return pltpu.make_async_remote_copy(
            src_ref=source, dst_ref=target, send_sem=send, recv_sem=recv,
            device_id=device, device_id_type=MESH,
        )

    def hop(stage, kind, unit):
        blocks_ref, all_ref = stages[stage]
        span = pl.ds(unit * GROUPS, GROUPS)
        odd = unit % 2
        if kind < 3:
            source, slot = blocks_ref.at[:, span], me
            target = (sibling, across, beside)[kind]
        elif kind == 3:
            slot, target = across, sibling
        elif kind == 4:
            slot, target = beside, sibling
        elif kind == 5:
            slot = across * (1 - odd) + beside * odd
            target = beside * (1 - odd) + across * odd
        else:
            slot, target = flip(across, 4), sibling
        place = all_ref.at[:, span, slot]
        if kind >= 3:
            source = place
        return remote(source, place, sent.at[stage, kind, unit], got.at[stage, kind, unit], (target, here))

    def own(stage, unit):
        blocks_ref, all_ref = stages[stage]
        span = pl.ds(unit * GROUPS, GROUPS)
        return pltpu.make_async_copy(
            blocks_ref.at[:, span], all_ref.at[:, span, me], own_sem.at[stage, unit]
        )

    def direct(stage, unit):
        for kind in (1, 2, 0):
            hop(stage, kind, unit).start()
        own(stage, unit).start()

    def forward(stage, unit):
        hop(stage, 1, unit).wait_recv()
        hop(stage, 2, unit).wait_recv()
        for kind in (5, 3, 4):
            hop(stage, kind, unit).start()

    def relay(stage, unit):
        hop(stage, 5, unit).wait_recv()
        hop(stage, 6, unit).start()

    def settle(stage, unit):
        for kind in (0, 3, 4, 6):
            hop(stage, kind, unit).wait_recv()
        own(stage, unit).wait()

    def advance(unit, stage):
        for step, action in ((AHEAD, direct), (2, forward), (1, relay)):
            if stage == 1:
                pl.when(unit + step < units)(functools.partial(action, 1, unit + step))
            else:
                pl.when(unit + step < units)(functools.partial(action, 0, unit + step))
                pl.when(unit + step >= units)(functools.partial(action, 1, unit + step - units))
        settle(stage, unit)

    def swap(bit, unit):
        cols = pl.ds(pl.multiple_of(unit * chunk, chunk), chunk)
        return remote(
            tokens.at[:, cols], swapped.at[bit, :, cols],
            tok_sent.at[bit, unit], tok_got.at[bit, unit], (me, flip(here, 1 << bit)),
        )

    def hand(bit, unit):
        cols = pl.ds(pl.multiple_of(unit * chunk, chunk), chunk)
        return remote(
            give.at[bit, :, cols], take.at[bit, :, cols],
            give_sent.at[bit, unit], give_got.at[bit, unit], (me, flip(here, 1 << bit)),
        )

    def scatter(which, k):
        there = (here + k) % slabs
        return remote(
            rank_part.at[which, pl.ds(pl.multiple_of(there * share, share), share)],
            rank_in.at[which, k - 1],
            rs_sent.at[which, k - 1], rs_got.at[which, k - 1], (me, there),
        )

    def gather(which, k):
        there = (here + k) % slabs
        mine = rank.at[which, pl.ds(pl.multiple_of(here * share, share), share)]
        return remote(mine, mine, ag_sent.at[which, k - 1], ag_got.at[which, k - 1], (me, there))

    def add_shares(which):
        for k in range(1, slabs):
            scatter(which, k).wait_recv()
        mine = pl.ds(pl.multiple_of(here * share, share), share)
        total = rank_part[which, mine, :]
        for k in range(1, slabs):
            total = total + rank_in[which, k - 1]
        rank[which, mine, :] = total.astype(jnp.bfloat16)
        for k in range(1, slabs):
            gather(which, k).start()

    pre = [
        pltpu.make_async_copy(source, target, pre_sem.at[i])
        for i, (source, target) in enumerate(((tokens, tok), (up_left, left), (down_right, right)))
    ]
    for copy in pre[:2]:
        copy.start()
    for unit in range(AHEAD):
        direct(0, unit)
    pre[2].start()
    for copy in pre[:2]:
        copy.wait()
    rank_part[0, :, :] = jnp.dot(tok[...], left[...], preferred_element_type=jnp.float32)
    for k in range(1, slabs):
        scatter(0, k).start()
    for unit in range(2):
        for bit in range(bits):
            swap(bit, unit).start()
    acc[...] = jnp.zeros_like(acc)
    rank_part[1, :, :] = jnp.zeros_like(rank_part[1])
    forward(0, 0)
    add_shares(0)
    for unit in range(2, units):
        for bit in range(bits):
            swap(bit, unit).start()
    relay(0, 0)
    forward(0, 1)
    for k in range(1, slabs):
        gather(0, k).wait_recv()

    tile = 256

    def up_unit(unit, carry):
        advance(unit, 0)
        loads = []
        for j in range(GROUPS):
            group = unit * GROUPS + j
            span = pl.ds(pl.multiple_of(group * width, width), width)
            loads.append((
                pltpu.make_async_copy(up_all.at[:, group], w_up.at[j], load_sem.at[0, j]),
                pltpu.make_async_copy(up_right.at[:, span], w_right.at[j], load_sem.at[1, j]),
                pltpu.make_async_copy(down_left.at[span], w_left.at[j], load_sem.at[2, j]),
            ))
        for trio in loads:
            for copy in trio:
                copy.start()
        for bit in range(bits):
            swap(bit, unit).wait_recv()
        for j in range(GROUPS):
            group = unit * GROUPS + j
            for copy in loads[j]:
                copy.wait()
            parts = []
            for term in range(terms):
                if term == 0:
                    at = group
                elif term < locals_:
                    at = flip(group, 1 << (term - 1))
                else:
                    at = group
                cols = pl.ds(pl.multiple_of(at * size, size), size)
                parts.append(tok[:, cols] if term < locals_ else swapped[term - locals_, :, cols])
            source = jnp.concatenate(parts, axis=1)
            coords = rank[0]
            for n in range(width // tile):
                cut = slice(n * tile, (n + 1) * tile)
                weights = w_up[j, :, :, :, cut].reshape(depth, tile)
                pre_act = jnp.dot(source, weights, preferred_element_type=jnp.float32)
                pre_act += jnp.dot(coords, w_right[j, :, cut], preferred_element_type=jnp.float32)
                value = 0.5 * pre_act * (1.0 + lax.erf(pre_act * (0.5 ** 0.5)))
                start = pl.multiple_of(group * width + n * tile, tile)
                active[:, pl.ds(start, tile)] = value.astype(jnp.bfloat16)
            span = pl.ds(pl.multiple_of(group * width, width), width)
            rank_part[1, :, :] += jnp.dot(
                active[:, span], w_left[j], preferred_element_type=jnp.float32
            )
        return carry

    lax.fori_loop(0, units, up_unit, 0)
    for k in range(1, slabs):
        scatter(1, k).start()
    pre[2].wait()

    def down_unit(unit, carry):
        advance(unit, 1)
        loads = [
            pltpu.make_async_copy(
                down_all.at[:, unit * GROUPS + j], w_down.at[j], load_sem.at[0, j]
            )
            for j in range(GROUPS)
        ]
        for copy in loads:
            copy.start()
        pl.when(unit == 2)(functools.partial(add_shares, 1))

        @pl.when(unit == 5)
        def _():
            for k in range(1, slabs):
                gather(1, k).wait_recv()
            for n in range(acc.shape[1] // 512):
                cut = slice(n * 512, (n + 1) * 512)
                acc[:, cut] += jnp.dot(rank[1], right[:, cut], preferred_element_type=jnp.float32)

        for j in range(GROUPS):
            group = unit * GROUPS + j
            loads[j].wait()
            span = pl.ds(pl.multiple_of(group * width, width), width)
            source = active[:, span]
            for first in range(0, terms, 2):
                pair = range(first, min(first + 2, terms))
                weights = jnp.concatenate(
                    [w_down[j, term].reshape(width, size) for term in pair], axis=1
                )
                product = jnp.dot(source, weights, preferred_element_type=jnp.float32)
                for term in pair:
                    piece = product[:, (term - first) * size : (term - first + 1) * size]
                    if term < locals_:
                        at = group if term == 0 else flip(group, 1 << (term - 1))
                        acc[:, pl.ds(pl.multiple_of(at * size, size), size)] += piece
                    else:
                        cols = pl.ds(pl.multiple_of(group * size, size), size)
                        give[term - locals_, :, cols] = piece.astype(jnp.bfloat16)
        for bit in range(bits):
            hand(bit, unit).start()
        return carry

    lax.fori_loop(0, units, down_unit, 0)

    def finish(unit, carry):
        cols = pl.ds(pl.multiple_of(unit * chunk, chunk), chunk)
        for bit in range(bits):
            hand(bit, unit).wait_recv()
        total = acc[:, cols]
        for bit in range(bits):
            total = total + take[bit, :, cols].astype(jnp.float32)
        out[:, cols] = total.astype(jnp.bfloat16)
        for stage in range(2):
            for kind in range(7):
                hop(stage, kind, unit).wait_send()
        for bit in range(bits):
            swap(bit, unit).wait_send()
            hand(bit, unit).wait_send()
        return carry

    lax.fori_loop(0, units, finish, 0)
    for which in range(2):
        for k in range(1, slabs):
            scatter(which, k).wait_send()
            gather(which, k).wait_send()


def shards_fused(tokens, up_blocks, up_left, up_right, down_blocks, down_left, down_right):
    rows, features = tokens.shape
    terms, blocks, up_rows, width = up_blocks.shape
    down_rows, size = down_blocks.shape[2:]
    rank = up_left.shape[1]
    count, slabs = lax.axis_size("dp"), lax.axis_size("hid")
    bits = slabs.bit_length() - 1
    units = blocks // GROUPS
    any_ = pl.BlockSpec(memory_space=pl.ANY)
    bf, f32 = jnp.bfloat16, jnp.float32
    dma = pltpu.SemaphoreType.DMA
    out, _, _ = pl.pallas_call(
        fused,
        out_shape=(
            jax.ShapeDtypeStruct((rows, features), bf),
            jax.ShapeDtypeStruct((terms, blocks, count, up_rows, width), bf),
            jax.ShapeDtypeStruct((terms, blocks, count, down_rows, size), bf),
        ),
        in_specs=[any_] * 7,
        out_specs=(pl.BlockSpec(memory_space=pltpu.VMEM), any_, any_),
        scratch_shapes=[
            pltpu.VMEM((rows, features), bf),
            pltpu.VMEM((bits, rows, features), bf),
            pltpu.VMEM((features, rank), bf),
            pltpu.VMEM((rank, features), bf),
            pltpu.VMEM((2, rows, rank), bf),
            pltpu.VMEM((2, rows, rank), f32),
            pltpu.VMEM((2, slabs - 1, rows // slabs, rank), f32),
            pltpu.VMEM((rows, blocks * width), bf),
            pltpu.VMEM((rows, features), f32),
            pltpu.VMEM((bits, rows, features), bf),
            pltpu.VMEM((bits, rows, features), bf),
            pltpu.VMEM((GROUPS, terms, count, up_rows, width), bf),
            pltpu.VMEM((GROUPS, rank, width), bf),
            pltpu.VMEM((GROUPS, terms, count, down_rows, size), bf),
            pltpu.VMEM((GROUPS, width, rank), bf),
            dma((2, 7, units)), dma((2, 7, units)),
            dma((bits, units)), dma((bits, units)),
            dma((bits, units)), dma((bits, units)),
            dma((2, slabs - 1)), dma((2, slabs - 1)),
            dma((2, slabs - 1)), dma((2, slabs - 1)),
            dma((2, units)), dma((3, GROUPS)), dma((3,)),
        ],
        compiler_params=pltpu.CompilerParams(
            collective_id=0, has_side_effects=True, vmem_limit_bytes=62 * 1024 * 1024
        ),
    )(tokens, up_blocks, up_left, up_right, down_blocks, down_left, down_right)
    return out


def shards(tokens, up_blocks, *rest):
    terms, blocks, up_rows, _ = up_blocks.shape
    slabs = lax.axis_size("hid")
    reach = blocks.bit_length() - 1 + slabs.bit_length()
    fits = (
        lax.axis_size("dp") == 8
        and up_rows % 16 == 0
        and blocks >= GROUPS * 6
        and blocks % GROUPS == 0
        and terms == reach
        and slabs > 1
        and tokens.shape[0] % (16 * slabs) == 0
    )
    body = shards_fused if fits else shards_plain
    return body(tokens, up_blocks, *rest)


def solution(mesh):
    placed = (
        P("dp", "hid"),
        P(None, "hid", "dp", None),
        P("hid", None),
        P(None, "hid"),
        P(None, "hid", "dp", None),
        P("hid", None),
        P(None, "hid"),
    )
    return jax.shard_map(
        shards, mesh=mesh, in_specs=placed, out_specs=P("dp", "hid"), check_vma=False
    )
```
